256 devices in a mesh: probe: 4 (over x), space: 64 (over y, z, core).
Axes of the slice: x: 4, y: 4, z: 8, core: 2. Of those that a mesh axis runs over, the one named last changes fastest.
Arguments:
- courant_field: float32 [128, 32, 256], P('space'), may hold values from 0.05 to 0.3
- probe_fields: float32 [16, 128, 32, 256], P('probe', 'space'), may hold values from -6 to 6
- prior_weight: float32 [128, 32, 256], P('space'), may hold values from 0.5 to 5
- source_cells: int32 [4096], P('space'), may hold values from 0 to 1048575, as said below
- source_strength: float32 [4096], P('space'), may hold values from -6 to 6
- wavelet: float32 [8], replicated, may hold values from -4 to 4
- receiver_cells: int32 [4096], P('space'), may hold values from 0 to 1048575, as said below
- receiver_weight: float32 [4096], P('space'), may hold values from 1 to 10
Outputs:
- hessian_fields: float32 [16, 128, 32, 256], P('probe', 'space')
- basis: float32 [16, 128, 32, 256], P('probe', 'space')
The draws below stay inside these ranges and needn't reach their ends.
Inputs may be any that keep to these rules, and one draw needn't show every extreme that they name: `source_cells`: entries k * 64 to (k + 1) * 64 - 1 are cells of the k-th slab of 2 planes along the first dimension; cells may repeat. `receiver_cells`: entries k * 64 to (k + 1) * 64 - 1 are cells of the k-th slab of 2 planes along the first dimension; cells may repeat.
All inputs are finite; a program needn't handle non-finite values.
Results may differ from the reference program's by a relative error of at most 0.0019.
Values sent between devices are 32-bit elements; how exact they have to be, the bound alone decides.
No kernel may reach another device: no remote copies, remote signals or barrier semaphores. Data moves between devices by JAX's collectives and lax.ppermute only.
A program may use at most 64 MiB of HBM per device.

```python
import math
import jax
import jax.numpy as jnp
from jax import lax

CX = 2
CY = 32
CZ = 256
NT = 8
RANK = 16
SRC_DEV = 64
REC_DEV = 64
NX = 128
NY = 32
NZ = 256
NSRC = 4096
NREC = 4096


def slab_cells(key, per_slab):
    slab_size = CX * CY * CZ
    slabs = NX // CX
    local_cells = jax.random.randint(key, (slabs, per_slab), 0, slab_size)
    starts = (jnp.arange(slabs, dtype=jnp.int32) * slab_size)[:, None]
    cells_all = (local_cells + starts).reshape(-1)
    cells_all = cells_all.at[0].set(0)
    cells_all = cells_all.at[-1].set(slabs * slab_size - 1)
    return cells_all.astype(jnp.int32)


def draw_source_cells(key, part):
    return slab_cells(jax.random.fold_in(key, 11), SRC_DEV)


def draw_receiver_cells(key, part):
    return slab_cells(jax.random.fold_in(key, 23), REC_DEV)


def block_scale(key, shape, shards, least, largest):
    def one(dim, parts):
        draws = jax.random.uniform(jax.random.fold_in(jax.random.fold_in(key, 6), dim), (parts,), jnp.float32, least / len(shards), largest / len(shards))
        return jnp.repeat(jnp.exp(draws), shape[dim] // parts).reshape((-1,) + (1,) * (len(shape) - dim - 1))

    factor_of = one(*shards[0])
    for cut in shards[1:]:
        factor_of = factor_of * one(*cut)
    return factor_of


def bell_draw(own_key, extent, deviation, reach, pieces=(), kind=jnp.bfloat16):
    array = jax.random.normal(own_key, extent, jnp.float32) * deviation
    if len(pieces) > 0:
        array = block_scale(own_key, extent, pieces, -0.22, 0.18) * array
    return jnp.clip(array, min=-reach, max=reach).astype(kind)


def setup_inputs(seed: int = 0) -> dict:
    arg_keys = jax.random.split(jax.random.key(seed), 9)
    return {
        "courant_field": jnp.clip(0.05 + 0.25 * jax.random.uniform(arg_keys[0], (NX, NY, NZ), jnp.float32) ** block_scale(arg_keys[0], (NX, NY, NZ), ((0, 64),), -0.2, 0.2), 0.05, 0.3),
        "probe_fields": bell_draw(arg_keys[1], (RANK, NX, NY, NZ), 1.0, 6.0, ((0, 4), (1, 64)), jnp.float32),
        "prior_weight": jnp.clip(jnp.exp(math.log(5.0) - 2.3025851 * jax.random.uniform(arg_keys[2], (NX, NY, NZ), jnp.float32) ** block_scale(arg_keys[2], (NX, NY, NZ), ((0, 64),), -0.2, 0.2)), 0.5, 5.0),
        "source_cells": draw_source_cells(jax.random.fold_in(arg_keys[8], 71), 0),
        "source_strength": bell_draw(arg_keys[4], (NSRC,), 1.0, 6.0, ((0, 64),), jnp.float32),
        "wavelet": bell_draw(arg_keys[5], (NT,), 1.0, 4.0, (), jnp.float32),
        "receiver_cells": draw_receiver_cells(jax.random.fold_in(arg_keys[8], 71), 0),
        "receiver_weight": jnp.clip(jnp.exp(math.log(10.0) - 2.3025851 * jax.random.uniform(arg_keys[7], (NREC,), jnp.float32) ** block_scale(arg_keys[7], (NREC,), ((0, 64),), -0.2, 0.2)), 1.0, 10.0),
    }


def laplace_grid(field):
    padded = jnp.pad(field, 1)
    total = padded[2:, 1:-1, 1:-1] + padded[:-2, 1:-1, 1:-1]
    total = total + padded[1:-1, 2:, 1:-1] + padded[1:-1, :-2, 1:-1]
    total = total + padded[1:-1, 1:-1, 2:] + padded[1:-1, 1:-1, :-2]
    return total - 6.0 * field

def reference(courant_field, probe_fields, prior_weight, source_cells, source_strength, wavelet, receiver_cells, receiver_weight):
    grid_shape = courant_field.shape
    total_cells = NX * NY * NZ
    source_field = jnp.zeros((total_cells,), jnp.float32).at[source_cells].add(source_strength).reshape(grid_shape)
    wave_prev = jnp.zeros(grid_shape, jnp.float32)
    wave_now = jnp.zeros(grid_shape, jnp.float32)
    drives = []
    for step in range(NT):
        drive = courant_field * laplace_grid(wave_now)
        wave_next = 2.0 * wave_now - wave_prev + drive + wavelet[step] * source_field
        drives.append(drive)
        wave_prev, wave_now = (wave_now, wave_next)

    def apply_hessian(probe):
        born_prev = jnp.zeros(grid_shape, jnp.float32)
        born_now = jnp.zeros(grid_shape, jnp.float32)
        records = []
        for step in range(NT):
            born_next = 2.0 * born_now - born_prev + courant_field * laplace_grid(born_now) + probe * drives[step]
            records.append(born_next.reshape(-1)[receiver_cells])
            born_prev, born_now = (born_now, born_next)
        adjoint_next = jnp.zeros(grid_shape, jnp.float32)
        adjoint_after = jnp.zeros(grid_shape, jnp.float32)
        hessian = prior_weight * probe
        for level in range(NT, 0, -1):
            injected = jnp.zeros((total_cells,), jnp.float32).at[receiver_cells].add(receiver_weight * records[level - 1]).reshape(grid_shape)
            adjoint_now = 2.0 * adjoint_next - adjoint_after + laplace_grid(courant_field * adjoint_next) + injected
            hessian = hessian + drives[level - 1] * adjoint_now
            adjoint_after, adjoint_next = (adjoint_next, adjoint_now)
        return hessian
    hessian_fields = lax.map(apply_hessian, probe_fields)
    rows = hessian_fields.reshape(RANK, total_cells)
    gram = lax.dot_general(rows.astype(jnp.float32), rows.astype(jnp.float32), (((1,), (1,)), ((), ())), precision=lax.Precision.HIGHEST, preferred_element_type=jnp.float32) / total_cells
    lower = jnp.linalg.cholesky(gram)
    basis = lax.linalg.triangular_solve(lower, rows, left_side=True, lower=True).reshape(hessian_fields.shape)
    return (hessian_fields, basis)
```

```python
import jax
import jax.numpy as jnp
from jax import lax
from jax.experimental import pallas as pl
from jax.experimental.pallas import tpu as pltpu
from jax.sharding import PartitionSpec as P


F32 = jnp.float32
BF16 = jnp.bfloat16
NY, NZ = 32, 256
OWN = 4
EXT = 5 * OWN
LIST = 8
VMEM = pl.BlockSpec(memory_space=pltpu.VMEM)
SMEM = pl.BlockSpec(memory_space=pltpu.SMEM)
NT_DIMS = (((1,), (1,)), ((), ()))
NN_DIMS = (((1,), (0,)), ((), ()))


def call(kernel, outs, n_in, scratch=(), smem=(), name=None, flops=0):
    shapes = [jax.ShapeDtypeStruct(s, F32) for s in outs]
    return pl.pallas_call(
        kernel,
        out_shape=shapes if len(shapes) > 1 else shapes[0],
        in_specs=[SMEM if i in smem else VMEM for i in range(n_in)],
        out_specs=[VMEM] * len(shapes) if len(shapes) > 1 else VMEM,
        scratch_shapes=list(scratch),
        compiler_params=pltpu.CompilerParams(vmem_limit_bytes=56 << 20),
        name=name,
    )


def core_of():
    return lax.rem(lax.axis_index("space"), 2)


def halves(x):
    hi = x.astype(BF16)
    lo = (x - hi.astype(F32)).astype(BF16)
    return hi, lo


def dot(a, b, dims):
    return lax.dot_general(a, b, dims, preferred_element_type=F32)


def one_hots(cells):
    cell = cells.astype(jnp.int32)
    count = cell.shape[1]
    row = lax.shift_right_logical(cell, 8)
    col = lax.bitwise_and(cell, NZ - 1)
    in_row = lax.broadcasted_iota(jnp.int32, (OWN * NY, count), 0) == row
    in_col = lax.broadcasted_iota(jnp.int32, (NZ, count), 0) == col
    return in_row, in_col.astype(F32).astype(BF16)


def make_laplace():
    y = lax.broadcasted_iota(jnp.int32, (NY, NZ), 0)
    z = lax.broadcasted_iota(jnp.int32, (NY, NZ), 1)
    y_lo, y_hi, z_lo, z_hi = y > 0, y < NY - 1, z > 0, z < NZ - 1

    def laplace(below, f, above):
        total = below + above
        total = total + jnp.where(y_lo, pltpu.roll(f, 1, 0), 0.0)
        total = total + jnp.where(y_hi, pltpu.roll(f, NY - 1, 0), 0.0)
        total = total + jnp.where(z_lo, pltpu.roll(f, 1, 1), 0.0)
        total = total + jnp.where(z_hi, pltpu.roll(f, NZ - 1, 1), 0.0)
        return total - 6.0 * f

    return laplace


def pack_pair(p, courant, src, strength, rec, weight, out):
    other = 2 * (1 - core_of())
    for i in range(2):
        out[64 * i : 64 * (i + 1), :] = p[other + i].reshape(64, NZ)
    out[128:192, :] = courant[...].reshape(64, NZ)
    chip_cell = (lax.axis_index("space") // 2) * (OWN * NY * NZ)
    out[192:200, :] = jnp.zeros((LIST, NZ), F32)
    out[192:193, 64:128] = (src[...] - chip_cell).astype(F32)
    out[193:194, 64:128] = strength[...]
    out[194:195, 64:128] = (rec[...] - chip_cell).astype(F32)
    out[195:196, 64:128] = weight[...]


def pack_chip(p, courant, src, strength, rec, weight, got, own, right, left):
    core = core_of()
    mine = pl.multiple_of(core * 64, 64)
    theirs = pl.multiple_of((1 - core) * 64, 64)
    for i in range(2):
        own[pl.ds(128 * i + mine, 64), :] = p[2 * core + i].reshape(64, NZ)
        own[pl.ds(128 * i + theirs, 64), :] = got[64 * i : 64 * (i + 1), :]
    own[pl.ds(256 + mine, 64), :] = courant[...].reshape(64, NZ)
    own[pl.ds(256 + theirs, 64), :] = got[128:192, :]
    chip_cell = (lax.axis_index("space") // 2) * (OWN * NY * NZ)
    own[384:392, :] = got[192:200, :]
    own[384:385, 0:64] = (src[...] - chip_cell).astype(F32)
    own[385:386, 0:64] = strength[...]
    own[386:387, 0:64] = (rec[...] - chip_cell).astype(F32)
    own[387:388, 0:64] = weight[...]
    for i in range(3):
        left[64 * i : 64 * (i + 1), :] = own[128 * i : 128 * i + 64, :]
        right[64 * i : 64 * (i + 1), :] = own[128 * i + 64 : 128 * i + 128, :]
    left[192:200, :] = own[384:392, :]
    right[192:200, :] = own[384:392, :]


def forward(
    own, l1, r1, l2, r2, wavelet, drives, wrec, courant, cells, src, wave, born, probe, drive
):
    chip = lax.axis_index("space") // 2
    last = lax.axis_size("space") // 2 - 1
    keep = [
        jnp.where(ok, 1.0, 0.0).astype(F32)
        for ok in (chip >= 2, chip >= 1, chip >= 0, chip <= last - 1, chip <= last - 2)
    ]
    slots = (l2, l1, own, r1, r2)
    lists = (192, 384, 384, 384, 192)
    cells[...] = jnp.zeros((LIST, 128), F32)
    for m, (ref, base) in enumerate(zip(slots, lists)):
        listed = ref[base : base + LIST, 0:128]
        in_row, in_col = one_hots(listed[0:1])
        strength = listed[1:2] * keep[m]
        hi, lo = halves(jnp.where(in_row, strength, 0.0))
        field = dot(hi, in_col, NT_DIMS) + dot(lo, in_col, NT_DIMS)
        src[4 * m : 4 * m + 4] = field.reshape(OWN, NY, NZ)
        cells[m : m + 1, :] = listed[2:3]
    for m, ref in ((1, l1), (2, own), (3, r1)):
        for i in range(2):
            probe[i, 4 * m : 4 * m + 4] = ref[128 * i : 128 * (i + 1), :].reshape(OWN, NY, NZ)
        courant[4 * m : 4 * m + 4] = keep[m] * ref[256:384, :].reshape(OWN, NY, NZ)
    for m, at, ref in ((0, 2, l2), (4, 16, r2)):
        for i in range(2):
            probe[i, at : at + 2] = ref[64 * i : 64 * (i + 1), :].reshape(2, NY, NZ)
        courant[at : at + 2] = keep[m] * ref[128:192, :].reshape(2, NY, NZ)
    zero = jnp.zeros((NY, NZ), F32)
    for e in (0, 1, 18, 19):
        courant[e] = zero
    first = wavelet[0]

    def start(e, _):
        wave[1, e] = first * src[e]
        wave[0, e] = zero
        for i in range(2):
            born[0, i, e] = zero
            born[1, i, e] = zero
        return 0

    lax.fori_loop(0, EXT, start, 0)
    laplace = make_laplace()
    listed = own[384:392, 0:128]
    in_row, in_col = one_hots(listed[2:3])
    row_mask = jnp.where(in_row, 1.0, 0.0)
    weight = listed[3:4]
    wrec[...] = jnp.zeros((16, 128), F32)
    for t in range(1, 8):
        now, nxt = t % 2, (t + 1) % 2
        pulse = wavelet[t]

        def advance(e, _, now=now, nxt=nxt, pulse=pulse, t=t):
            c = courant[e]
            w = wave[now, e]
            d = c * laplace(wave[now, e - 1], w, wave[now, e + 1])
            drive[e] = d
            if t < 7:
                wave[nxt, e] = 2.0 * w - wave[nxt, e] + d + pulse * src[e]
            for i in range(2):
                force = probe[i, e] * d
                if t > 1:
                    b = born[now, i, e]
                    bent = laplace(born[now, i, e - 1], b, born[now, i, e + 1])
                    force = force + (2.0 * b - born[nxt, i, e] + c * bent)
                born[nxt, i, e] = force
            return 0

        lax.fori_loop(1 + t, 19 - t, advance, 0)
        drives[t - 1] = drive[8:12]
        for i in range(2):
            hi, lo = halves(born[nxt, i, 8:12].reshape(OWN * NY, NZ))
            picked = dot(hi, in_col, NN_DIMS) + dot(lo, in_col, NN_DIMS)
            value = jnp.sum(picked * row_mask, axis=0, keepdims=True)
            at = 2 * (t - 1) + i
            wrec[at : at + 1, :] = value * weight


def adjoint(courant, cells, w2l, w1l, w0, w1r, w2r, drives, mine, send, inj, adj, bent, hess):
    recs = (w2l, w1l, w0, w1r, w2r)
    for m, ref in enumerate(recs):
        in_row, in_col = one_hots(cells[m : m + 1, :])
        for k in range(8, 1, -1):
            lo_e, hi_e = 10 - k, 9 + k
            if 4 * m + 3 < lo_e or 4 * m > hi_e:
                continue
            for i in range(2):
                at = 2 * (k - 2) + i
                hi, lo = halves(ref[at : at + 1, :])
                a = jnp.where(in_row, hi.astype(F32), 0.0).astype(BF16)
                b = jnp.where(in_row, lo.astype(F32), 0.0).astype(BF16)
                field = dot(a, in_col, NT_DIMS) + dot(b, in_col, NT_DIMS)
                inj[k - 2, i, 4 * m : 4 * m + 4] = field.reshape(OWN, NY, NZ)
    laplace = make_laplace()

    def begin(e, _):
        for i in range(2):
            a = inj[6, i, e]
            adj[0, i, e] = a
            bent[0, i, e] = courant[e] * a
        return 0

    lax.fori_loop(2, 18, begin, 0)
    for i in range(2):
        for e in range(OWN):
            hess[i, e] = drives[6, e] * adj[0, i, 8 + e]
    for k in range(7, 1, -1):
        now, nxt = k % 2, (k + 1) % 2

        def advance(e, _, k=k, now=now, nxt=nxt):
            for i in range(2):
                a = 2.0 * adj[nxt, i, e] + inj[k - 2, i, e]
                a = a + laplace(bent[nxt, i, e - 1], bent[nxt, i, e], bent[nxt, i, e + 1])
                if k < 7:
                    a = a - adj[now, i, e]
                adj[now, i, e] = a
                if k > 2:
                    bent[now, i, e] = courant[e] * a
            return 0

        lax.fori_loop(10 - k, 10 + k, advance, 0)
        for i in range(2):
            for e in range(OWN):
                hess[i, e] = hess[i, e] + drives[k - 2, e] * adj[now, i, 8 + e]
    core = core_of()
    for i in range(2):
        for e in range(2):
            mine[i, e] = hess[i, 2 * core + e]
            send[i, e] = hess[i, 2 * (1 - core) + e]


def finish(p, prior, mine, got, out):
    core = core_of()
    for i in range(2):
        out[2 * core + i] = prior[...] * p[2 * core + i] + mine[i]
        out[2 * (1 - core) + i] = prior[...] * p[2 * (1 - core) + i] + got[i]


def gram_part(h0, h1, h2, h3, out, sums):
    group = lax.axis_index("probe")
    blocks = (h0, h1, h2, h3)
    start = [lax.rem(group + 4 - b, 4) * 4 for b in range(4)]
    for a in range(4):
        for b in range(a, 4):
            pairs = [(i, j) for i in range(4) for j in range(4) if a != b or i <= j]
            acc = [None] * len(pairs)
            for plane in range(2):
                for y in range(0, NY, 8):
                    left = [blocks[a][i, plane, y : y + 8, :] for i in range(4)]
                    right = [blocks[b][j, plane, y : y + 8, :] for j in range(4)] if a != b else left
                    for n, (i, j) in enumerate(pairs):
                        prod = left[i] * right[j]
                        prod = prod[:, :128] + prod[:, 128:]
                        acc[n] = prod if acc[n] is None else acc[n] + prod
            for n, (i, j) in enumerate(pairs):
                total = jnp.sum(acc[n], axis=0, keepdims=True)
                row, col = start[a] + i, start[b] + j
                sums[pl.ds(row * 16 + col, 1), :] = total
                sums[pl.ds(col * 16 + row, 1), :] = total
    flat = lax.dot_general(
        jnp.ones((8, 128), F32),
        sums[...],
        NT_DIMS,
        precision=lax.Precision.HIGHEST,
        preferred_element_type=F32,
    )
    pair = jnp.concatenate([flat[0:1, :128], flat[0:1, 128:]], axis=0)
    out[...] = jnp.broadcast_to(pair[None], out.shape)


def whiten(scale, parts, h0, h1, h2, h3, out, work):
    exact = dict(precision=lax.Precision.HIGHEST, preferred_element_type=F32)
    group = lax.axis_index("probe")
    total = jnp.sum(parts[...], axis=0) * scale
    row = lax.broadcasted_iota(jnp.int32, (16, 128), 0)
    lane = lax.broadcasted_iota(jnp.int32, (16, 128), 1)
    spread = jnp.where(
        row < 8,
        jnp.broadcast_to(total[0:1], (16, 128)),
        jnp.broadcast_to(total[1:2], (16, 128)),
    )
    spread = jnp.where(lax.shift_right_logical(lane, 4) == lax.bitwise_and(row, 7), spread, 0.0)
    from_lane = lax.broadcasted_iota(jnp.int32, (128, 128), 0)
    to_lane = lax.broadcasted_iota(jnp.int32, (128, 128), 1)
    select = jnp.where(lax.bitwise_and(from_lane, 15) == to_lane, 1.0, 0.0)
    x = lax.dot_general(spread, select, NN_DIMS, **exact)
    x = x + jnp.where(lane == row + 16, 1.0, 0.0)
    for k in range(16):
        column = jnp.broadcast_to(x[:, k : k + 1], (16, 128))
        pivot = jnp.broadcast_to(column[k : k + 1], (16, 128))
        ratio = jnp.broadcast_to(x[k : k + 1], (16, 128)) / pivot
        x = jnp.where(row > k, x - column * ratio, x)
        x = jnp.where(row == k, x * lax.rsqrt(pivot), x)
    work[...] = x
    rows = work[pl.ds(pl.multiple_of(group * 4, 4), 4), :]
    rows = jnp.concatenate([rows, rows], axis=0)
    block = lax.bitwise_and(group + 4 - lax.shift_right_logical(to_lane, 2), 3)
    source = 16 + block * 4 + lax.bitwise_and(to_lane, 3)
    order = jnp.where(jnp.logical_and(from_lane == source, to_lane < 16), 1.0, 0.0)
    coef = lax.dot_general(rows, order, NN_DIMS, **exact)
    blocks = (h0, h1, h2, h3)
    for r in range(4):
        c = [jnp.broadcast_to(coef[r : r + 1, s : s + 1], (8, NZ)) for s in range(16)]
        for plane in range(2):
            for y in range(0, NY, 8):
                acc = None
                for s in range(16):
                    term = c[s] * blocks[s // 4][s % 4, plane, y : y + 8, :]
                    acc = term if acc is None else acc + term
                out[r, plane, y : y + 8, :] = acc


def shards(
    courant_field,
    probe_fields,
    prior_weight,
    source_cells,
    source_strength,
    wavelet,
    receiver_cells,
    receiver_weight,
):
    count = lax.axis_size("space")
    lists = [
        v.reshape(1, -1) for v in (source_cells, source_strength, receiver_cells, receiver_weight)
    ]

    def swap(x):
        return lax.ppermute(x, "space", [(i, i ^ 1) for i in range(count)])

    def shift(x, by):
        return lax.ppermute(x, "space", [(i, (i + by) % count) for i in range(count)])

    pair = call(pack_pair, [(200, NZ)], 6, name="pack_pair")(probe_fields, courant_field, *lists)
    got = swap(pair)
    own, right, left = call(
        pack_chip, [(392, NZ), (200, NZ), (200, NZ)], 7, name="pack_chip"
    )(probe_fields, courant_field, *lists, got)
    l1, r1 = shift(own, 2), shift(own, -2)
    l2, r2 = shift(right, 4), shift(left, -4)
    plane = (NY, NZ)
    drives, wrec, courant, cells = call(
        forward,
        [(7, OWN) + plane, (16, 128), (EXT,) + plane, (LIST, 128)],
        6,
        scratch=[
            pltpu.VMEM((EXT,) + plane, F32),
            pltpu.VMEM((2, EXT) + plane, F32),
            pltpu.VMEM((2, 2, EXT) + plane, F32),
            pltpu.VMEM((2, EXT) + plane, F32),
            pltpu.VMEM((EXT,) + plane, F32),
        ],
        smem=(5,),
        name="forward",
    )(own, l1, r1, l2, r2, wavelet)
    w1l, w1r, w2l, w2r = shift(wrec, 2), shift(wrec, -2), shift(wrec, 4), shift(wrec, -4)
    half = (2, 2) + plane
    mine, send = call(
        adjoint,
        [half, half],
        8,
        scratch=[
            pltpu.VMEM((7, 2, EXT) + plane, F32),
            pltpu.VMEM((2, 2, EXT) + plane, F32),
            pltpu.VMEM((2, 2, EXT) + plane, F32),
            pltpu.VMEM((2, OWN) + plane, F32),
        ],
        name="adjoint",
    )(courant, cells, w2l, w1l, wrec, w1r, w2r, drives)
    hessian = call(finish, [(4, 2) + plane], 4, name="finish")(
        probe_fields, prior_weight, mine, swap(send)
    )
    groups = lax.axis_size("probe")
    others = [
        lax.ppermute(hessian, "probe", [(i, (i + b) % groups) for i in range(groups)])
        for b in (1, 2, 3)
    ]
    part = call(
        gram_part, [(count, 2, 128)], 4, scratch=[pltpu.VMEM((256, 128), F32)], name="gram"
    )(hessian, *others)
    parts = lax.all_to_all(part, "space", 0, 0, tiled=True)
    scale = 1.0 / (count * hessian[0].size)

    def whiten_scaled(*refs):
        whiten(scale, *refs)

    basis = call(
        whiten_scaled, [(4, 2) + plane], 5, scratch=[pltpu.VMEM((16, 128), F32)], name="whiten"
    )(parts, hessian, *others)
    return (hessian, basis)


def solution(mesh):
    in_specs = (
        P("space", None, None),
        P("probe", "space", None, None),
        P("space", None, None),
        P("space"),
        P("space"),
        P(),
        P("space"),
        P("space"),
    )
    out_specs = (P("probe", "space", None, None), P("probe", "space", None, None))
    return jax.shard_map(shards, mesh=mesh, in_specs=in_specs, out_specs=out_specs, check_vma=False)
```

```python
import jax
import jax.numpy as jnp
from jax import lax
from jax.experimental import pallas as pl
from jax.experimental.pallas import tpu as pltpu
from jax.sharding import PartitionSpec as P


F32 = jnp.float32
BF16 = jnp.bfloat16
NY, NZ = 32, 256
OWN = 4
EXT = 5 * OWN
LIST = 8
UNROLL = True
VMEM = pl.BlockSpec(memory_space=pltpu.VMEM)
SMEM = pl.BlockSpec(memory_space=pltpu.SMEM)
NT_DIMS = (((1,), (1,)), ((), ()))
NN_DIMS = (((1,), (0,)), ((), ()))


def call(kernel, outs, n_in, scratch=(), smem=(), name=None, mib=8):
    shapes = [jax.ShapeDtypeStruct(s, F32) for s in outs]
    return pl.pallas_call(
        kernel,
        out_shape=shapes if len(shapes) > 1 else shapes[0],
        in_specs=[SMEM if i in smem else VMEM for i in range(n_in)],
        out_specs=[VMEM] * len(shapes) if len(shapes) > 1 else VMEM,
        scratch_shapes=list(scratch),
        compiler_params=pltpu.CompilerParams(vmem_limit_bytes=mib << 20),
        name=name,
    )


def core_of():
    return lax.rem(lax.axis_index("space"), 2)


def halves(x):
    hi = x.astype(BF16)
    lo = (x - hi.astype(F32)).astype(BF16)
    return hi, lo


def dot(a, b, dims):
    return lax.dot_general(a, b, dims, preferred_element_type=F32)


def one_hots(cells):
    cell = cells.astype(jnp.int32)
    count = cell.shape[1]
    row = lax.shift_right_logical(cell, 8)
    col = lax.bitwise_and(cell, NZ - 1)
    in_row = lax.broadcasted_iota(jnp.int32, (OWN * NY, count), 0) == row
    in_col = lax.broadcasted_iota(jnp.int32, (NZ, count), 0) == col
    return in_row, in_col.astype(F32).astype(BF16)


def tiles_of(ref, *index):
    return [
        [ref[index + (slice(y, y + 8), slice(z, z + 128))] for z in range(0, NZ, 128)]
        for y in range(0, NY, 8)
    ]


def put_tile(ref, index, j, h, value):
    ref[index + (slice(8 * j, 8 * j + 8), slice(128 * h, 128 * h + 128))] = value


def make_laplace():
    y = lax.broadcasted_iota(jnp.int32, (8, 128), 0)
    z = lax.broadcasted_iota(jnp.int32, (8, 128), 1)
    y_lo, y_hi, z_lo, z_hi = y == 0, y == 7, z == 0, z == 127
    zero = jnp.zeros((8, 128), F32)

    def laplace(below, f, above):
        rows, cols = len(f), len(f[0])

        def shifted(axis, by):
            return [[pltpu.roll(v, by, axis) for v in line] for line in f]

        up, down, left, right = shifted(0, 1), shifted(0, 7), shifted(1, 1), shifted(1, 127)
        out = []
        for j in range(rows):
            line = []
            for h in range(cols):
                total = below[j][h] + above[j][h]
                side = jnp.where(y_lo, up[j - 1][h] if j > 0 else zero, up[j][h])
                total = total + side
                side = jnp.where(y_hi, down[j + 1][h] if j + 1 < rows else zero, down[j][h])
                total = total + side
                side = jnp.where(z_lo, left[j][h - 1] if h > 0 else zero, left[j][h])
                total = total + side
                side = jnp.where(z_hi, right[j][h + 1] if h + 1 < cols else zero, right[j][h])
                total = total + side
                line.append(total - 6.0 * f[j][h])
            out.append(line)
        return out

    return laplace


TILES = [(j, h) for j in range(NY // 8) for h in range(NZ // 128)]


def pack(courant, src, strength, rec, weight, out):
    chip_cell = (lax.axis_index("space") // 2) * (OWN * NY * NZ)
    out[0:64, :] = courant[...].reshape(64, NZ)
    out[64:72, :] = jnp.zeros((LIST, NZ), F32)
    out[64:65, 0:64] = (src[...] - chip_cell).astype(F32)
    out[65:66, 0:64] = strength[...]
    out[66:67, 0:64] = (rec[...] - chip_cell).astype(F32)
    out[67:68, 0:64] = weight[...]


def both_lists(own, got, core):
    first = core == 0
    low = jnp.where(first, own, got)
    high = jnp.where(first, got, own)
    return low[:, 0:128] + pltpu.roll(high[:, 0:128], 64, 1)


def forward(
    p,
    p_got,
    cl,
    cl_got,
    near,
    far,
    near_got,
    far_got,
    wavelet,
    drives,
    wrec,
    courant,
    cells,
    src,
    wave,
    born,
    probe,
    drive,
    table,
):
    core = core_of()
    back = 1 - core
    chip = lax.axis_index("space") // 2
    last = lax.axis_size("space") // 2 - 1
    lo1, lo2 = chip >= 1, chip >= 2
    hi1, hi2 = chip <= last - 1, chip <= last - 2
    first = core == 0

    def factor(ok):
        return jnp.where(ok, 1.0, 0.0).astype(F32)

    keep_near = factor(jnp.where(first, lo1, hi1))
    keep_far = factor(jnp.where(first, lo2, hi2))
    keep_near_got = factor(jnp.where(first, hi1, lo1))
    keep_far_got = factor(jnp.where(first, hi2, lo2))
    one = jnp.float32(1.0)

    def put_list(slot, low, high, side, scale):
        listed = both_lists(low, high, side)
        at = pl.multiple_of(slot * LIST, LIST)
        table[pl.ds(at, LIST), :] = listed
        table[pl.ds(at + 1, 1), :] = scale * listed[1:2]

    put_list(2, cl[64:72, :], cl_got[64:72, :], core, one)
    put_list(1 + 2 * core, near[576:584, :], near[648:656, :], core, keep_near)
    put_list(3 - 2 * core, near_got[576:584, :], near_got[648:656, :], back, keep_near_got)
    put_list(4 * core, far[328:336, :], far[320:328, :], core, keep_far)
    put_list(4 - 4 * core, far_got[328:336, :], far_got[320:328, :], back, keep_far_got)

    def put_planes(at, ref, p_row, c_row, scale):
        for i in range(2):
            row = pl.multiple_of(p_row + 128 * core + 64 * i, 64)
            probe[i, pl.ds(at, 2)] = ref[pl.ds(row, 64), :].reshape(2, NY, NZ)
        courant[pl.ds(at, 2)] = scale * ref[c_row : c_row + 64, :].reshape(2, NY, NZ)

    for i in range(2):
        probe[i, pl.ds(8 + 2 * core, 2)] = p[2 * core + i]
        probe[i, pl.ds(8 + 2 * back, 2)] = p_got[2 * core + i]
    courant[pl.ds(8 + 2 * core, 2)] = cl[0:64, :].reshape(2, NY, NZ)
    courant[pl.ds(8 + 2 * back, 2)] = cl_got[0:64, :].reshape(2, NY, NZ)
    base, base_got = 4 + 8 * core, 12 - 8 * core
    put_planes(base + 2 * core, near, 0, 512, keep_near)
    put_planes(base + 2 * back, near, 256, 584, keep_near)
    put_planes(base_got + 2 * back, near_got, 0, 512, keep_near_got)
    put_planes(base_got + 2 * core, near_got, 256, 584, keep_near_got)
    put_planes(2 + 14 * core, far, 0, 256, keep_far)
    put_planes(16 - 14 * core, far_got, 0, 256, keep_far_got)
    zero = jnp.zeros((NY, NZ), F32)
    for e in (0, 1, 18, 19):
        courant[e] = zero
    cells[...] = jnp.zeros((LIST, 128), F32)
    for m in range(5):
        listed = table[LIST * m : LIST * (m + 1), :]
        in_row, in_col = one_hots(listed[0:1])
        hi, lo = halves(jnp.where(in_row, listed[1:2], 0.0))
        field = dot(hi, in_col, NT_DIMS) + dot(lo, in_col, NT_DIMS)
        src[4 * m : 4 * m + 4] = field.reshape(OWN, NY, NZ)
        cells[m : m + 1, :] = listed[2:3]
    pulse_0 = wavelet[0]

    def start(e, _):
        wave[1, e] = pulse_0 * src[e]
        wave[0, e] = zero
        for i in range(2):
            born[0, i, e] = zero
            born[1, i, e] = zero
        return 0

    lax.fori_loop(0, EXT, start, 0)
    laplace = make_laplace()
    listed = table[2 * LIST : 3 * LIST, :]
    in_row, in_col = one_hots(listed[2:3])
    row_mask = jnp.where(in_row, 1.0, 0.0)
    weight = listed[3:4]
    wrec[...] = jnp.zeros((16, 128), F32)
    for t in range(1, 8):
        now, nxt = t % 2, (t + 1) % 2
        pulse = wavelet[t]

        def advance(e, _, now=now, nxt=nxt, pulse=pulse, t=t):
            c = tiles_of(courant, e)
            w = tiles_of(wave, now, e)
            d = laplace(tiles_of(wave, now, e - 1), w, tiles_of(wave, now, e + 1))
            for j, h in TILES:
                d[j][h] = c[j][h] * d[j][h]
                put_tile(drive, (e,), j, h, d[j][h])
            if t < 7:
                w_old, s = tiles_of(wave, nxt, e), tiles_of(src, e)
                for j, h in TILES:
                    w_new = 2.0 * w[j][h] - w_old[j][h] + d[j][h] + pulse * s[j][h]
                    put_tile(wave, (nxt, e), j, h, w_new)
            for i in range(2):
                q = tiles_of(probe, i, e)
                if t > 1:
                    b = tiles_of(born, now, i, e)
                    bent = laplace(
                        tiles_of(born, now, i, e - 1), b, tiles_of(born, now, i, e + 1)
                    )
                    b_old = tiles_of(born, nxt, i, e)
                for j, h in TILES:
                    b_new = q[j][h] * d[j][h]
                    if t > 1:
                        moved = 2.0 * b[j][h] - b_old[j][h] + c[j][h] * bent[j][h]
                        b_new = b_new + moved
                    put_tile(born, (nxt, i, e), j, h, b_new)
            return 0

        lax.fori_loop(1 + t, 19 - t, advance, 0, unroll=UNROLL)
        drives[t - 1] = drive[8:12]
        for i in range(2):
            hi, lo = halves(born[nxt, i, 8:12].reshape(OWN * NY, NZ))
            picked = dot(hi, in_col, NN_DIMS) + dot(lo, in_col, NN_DIMS)
            value = jnp.sum(picked * row_mask, axis=0, keepdims=True)
            at = 2 * (t - 1) + i
            wrec[at : at + 1, :] = value * weight


def adjoint(
    courant, cells, w0, near, far, near_got, far_got, drives, mine, send, inj, adj, bent, hess
):
    first = core_of() == 0
    side = [near[0:16, :], near_got[16:32, :], far[0:16, :], far_got[16:32, :]]
    recs = (
        jnp.where(first, side[2], side[3]),
        jnp.where(first, side[0], side[1]),
        w0[...],
        jnp.where(first, side[1], side[0]),
        jnp.where(first, side[3], side[2]),
    )
    for m, rec in enumerate(recs):
        in_row, in_col = one_hots(cells[m : m + 1, :])
        for k in range(8, 1, -1):
            lo_e, hi_e = 10 - k, 9 + k
            if 4 * m + 3 < lo_e or 4 * m > hi_e:
                continue
            for i in range(2):
                at = 2 * (k - 2) + i
                hi, lo = halves(rec[at : at + 1, :])
                a = jnp.where(in_row, hi.astype(F32), 0.0).astype(BF16)
                b = jnp.where(in_row, lo.astype(F32), 0.0).astype(BF16)
                field = dot(a, in_col, NT_DIMS) + dot(b, in_col, NT_DIMS)
                inj[k - 2, i, 4 * m : 4 * m + 4] = field.reshape(OWN, NY, NZ)
    laplace = make_laplace()

    def begin(e, _):
        for i in range(2):
            a = inj[6, i, e]
            adj[0, i, e] = a
            bent[0, i, e] = courant[e] * a
        return 0

    lax.fori_loop(2, 18, begin, 0)
    for i in range(2):
        for e in range(OWN):
            hess[i, e] = drives[6, e] * adj[0, i, 8 + e]
    for k in range(7, 1, -1):
        now, nxt = k % 2, (k + 1) % 2

        def advance(e, _, k=k, now=now, nxt=nxt):
            c = tiles_of(courant, e)
            for i in range(2):
                a_new = laplace(
                    tiles_of(bent, nxt, i, e - 1),
                    tiles_of(bent, nxt, i, e),
                    tiles_of(bent, nxt, i, e + 1),
                )
                a, a_old = tiles_of(adj, nxt, i, e), tiles_of(adj, now, i, e)
                pushed = tiles_of(inj, k - 2, i, e)
                for j, h in TILES:
                    value = a_new[j][h] + (2.0 * a[j][h] + pushed[j][h])
                    if k < 7:
                        value = value - a_old[j][h]
                    put_tile(adj, (now, i, e), j, h, value)
                    if k > 2:
                        put_tile(bent, (now, i, e), j, h, c[j][h] * value)
            return 0

        lax.fori_loop(10 - k, 10 + k, advance, 0, unroll=UNROLL)
        for i in range(2):
            for e in range(OWN):
                hess[i, e] = hess[i, e] + drives[k - 2, e] * adj[now, i, 8 + e]
    core = core_of()
    for i in range(2):
        for e in range(2):
            mine[i, e] = hess[i, 2 * core + e]
            send[i, e] = hess[i, 2 * (1 - core) + e]


def finish(p, prior, mine, got, out):
    core = core_of()
    for i in range(2):
        out[2 * core + i] = prior[...] * p[2 * core + i] + mine[i]
        out[2 * (1 - core) + i] = prior[...] * p[2 * (1 - core) + i] + got[i]


def gram_part(h0, h1, h2, h3, out, sums):
    group = lax.axis_index("probe")
    blocks = (h0, h1, h2, h3)
    start = [lax.rem(group + 4 - b, 4) * 4 for b in range(4)]
    for a in range(4):
        for b in range(a, 4):
            pairs = [(i, j) for i in range(4) for j in range(4) if a != b or i <= j]
            acc = [None] * len(pairs)
            for plane in range(2):
                for y in range(0, NY, 8):
                    left = [blocks[a][i, plane, y : y + 8, :] for i in range(4)]
                    right = [blocks[b][j, plane, y : y + 8, :] for j in range(4)] if a != b else left
                    for n, (i, j) in enumerate(pairs):
                        prod = left[i] * right[j]
                        prod = prod[:, :128] + prod[:, 128:]
                        acc[n] = prod if acc[n] is None else acc[n] + prod
            for n, (i, j) in enumerate(pairs):
                total = jnp.sum(acc[n], axis=0, keepdims=True)
                row, col = start[a] + i, start[b] + j
                sums[pl.ds(row * 16 + col, 1), :] = total
                sums[pl.ds(col * 16 + row, 1), :] = total
    flat = lax.dot_general(
        jnp.ones((8, 128), F32),
        sums[...],
        NT_DIMS,
        precision=lax.Precision.HIGHEST,
        preferred_element_type=F32,
    )
    pair = jnp.concatenate([flat[0:1, :128], flat[0:1, 128:]], axis=0)
    out[...] = jnp.broadcast_to(pair[None], out.shape)


def whiten(scale, parts, h0, h1, h2, h3, out, work):
    exact = dict(precision=lax.Precision.HIGHEST, preferred_element_type=F32)
    group = lax.axis_index("probe")
    total = jnp.sum(parts[...], axis=0) * scale
    row = lax.broadcasted_iota(jnp.int32, (16, 128), 0)
    lane = lax.broadcasted_iota(jnp.int32, (16, 128), 1)
    spread = jnp.where(
        row < 8,
        jnp.broadcast_to(total[0:1], (16, 128)),
        jnp.broadcast_to(total[1:2], (16, 128)),
    )
    spread = jnp.where(lax.shift_right_logical(lane, 4) == lax.bitwise_and(row, 7), spread, 0.0)
    from_lane = lax.broadcasted_iota(jnp.int32, (128, 128), 0)
    to_lane = lax.broadcasted_iota(jnp.int32, (128, 128), 1)
    select = jnp.where(lax.bitwise_and(from_lane, 15) == to_lane, 1.0, 0.0)
    x = lax.dot_general(spread, select, NN_DIMS, **exact)
    x = x + jnp.where(lane == row + 16, 1.0, 0.0)
    for k in range(16):
        column = jnp.broadcast_to(x[:, k : k + 1], (16, 128))
        pivot = jnp.broadcast_to(column[k : k + 1], (16, 128))
        ratio = jnp.broadcast_to(x[k : k + 1], (16, 128)) / pivot
        x = jnp.where(row > k, x - column * ratio, x)
        x = jnp.where(row == k, x * lax.rsqrt(pivot), x)
    work[...] = x
    rows = work[pl.ds(pl.multiple_of(group * 4, 4), 4), :]
    rows = jnp.concatenate([rows, rows], axis=0)
    block = lax.bitwise_and(group + 4 - lax.shift_right_logical(to_lane, 2), 3)
    source = 16 + block * 4 + lax.bitwise_and(to_lane, 3)
    order = jnp.where(jnp.logical_and(from_lane == source, to_lane < 16), 1.0, 0.0)
    coef = lax.dot_general(rows, order, NN_DIMS, **exact)
    blocks = (h0, h1, h2, h3)
    for r in range(4):
        c = [jnp.broadcast_to(coef[r : r + 1, s : s + 1], (8, NZ)) for s in range(16)]
        for plane in range(2):
            for y in range(0, NY, 8):
                acc = None
                for s in range(16):
                    term = c[s] * blocks[s // 4][s % 4, plane, y : y + 8, :]
                    acc = term if acc is None else acc + term
                out[r, plane, y : y + 8, :] = acc


def shards(
    courant_field,
    probe_fields,
    prior_weight,
    source_cells,
    source_strength,
    wavelet,
    receiver_cells,
    receiver_weight,
):
    count = lax.axis_size("space")
    def swap(x):
        return lax.ppermute(x, "space", [(i, i ^ 1) for i in range(count)])

    def inward(x, by):
        pairs = [(i, (i + (by if i % 2 == 0 else -by)) % count) for i in range(count)]
        return lax.ppermute(x, "space", pairs)

    p = probe_fields
    lists = [
        v.reshape(1, -1) for v in (source_cells, source_strength, receiver_cells, receiver_weight)
    ]
    cl = call(pack, [(72, NZ)], 5, name="pack")(courant_field, *lists)
    p_got, cl_got = swap(p), swap(cl)
    flat = p_got.reshape(256, NZ)
    near = inward(jnp.concatenate([p.reshape(256, NZ), flat, cl, cl_got], axis=0), 2)
    far = inward(jnp.concatenate([flat, cl_got, cl[64:72]], axis=0), 4)
    near_got, far_got = swap(near), swap(far)
    plane = (NY, NZ)
    drives, wrec, courant, cells = call(
        forward,
        [(7, OWN) + plane, (16, 128), (EXT,) + plane, (LIST, 128)],
        9,
        scratch=[
            pltpu.VMEM((EXT,) + plane, F32),
            pltpu.VMEM((2, EXT) + plane, F32),
            pltpu.VMEM((2, 2, EXT) + plane, F32),
            pltpu.VMEM((2, EXT) + plane, F32),
            pltpu.VMEM((EXT,) + plane, F32),
            pltpu.VMEM((5 * LIST, 128), F32),
        ],
        smem=(8,),
        name="forward",
        mib=16,
    )(p, p_got, cl, cl_got, near, far, near_got, far_got, wavelet)
    all_rec = jnp.concatenate([wrec, swap(wrec)], axis=0)
    rec_near, rec_far = inward(all_rec, 2), inward(all_rec, 4)
    rec_near_got, rec_far_got = swap(rec_near), swap(rec_far)
    half = (2, 2) + plane
    mine, send = call(
        adjoint,
        [half, half],
        8,
        scratch=[
            pltpu.VMEM((7, 2, EXT) + plane, F32),
            pltpu.VMEM((2, 2, EXT) + plane, F32),
            pltpu.VMEM((2, 2, EXT) + plane, F32),
            pltpu.VMEM((2, OWN) + plane, F32),
        ],
        name="adjoint",
        mib=24,
    )(courant, cells, wrec, rec_near, rec_far, rec_near_got, rec_far_got, drives)
    hessian = call(finish, [(4, 2) + plane], 4, name="finish")(
        probe_fields, prior_weight, mine, swap(send)
    )
    groups = lax.axis_size("probe")
    others = [
        lax.ppermute(hessian, "probe", [(i, (i + b) % groups) for i in range(groups)])
        for b in (1, 2, 3)
    ]
    part = call(
        gram_part, [(count, 2, 128)], 4, scratch=[pltpu.VMEM((256, 128), F32)], name="gram"
    )(hessian, *others)
    parts = lax.all_to_all(part, "space", 0, 0, tiled=True)
    scale = 1.0 / (count * hessian[0].size)

    def whiten_scaled(*refs):
        whiten(scale, *refs)

    basis = call(
        whiten_scaled, [(4, 2) + plane], 5, scratch=[pltpu.VMEM((16, 128), F32)], name="whiten"
    )(parts, hessian, *others)
    return (hessian, basis)


def solution(mesh):
    in_specs = (
        P("space", None, None),
        P("probe", "space", None, None),
        P("space", None, None),
        P("space"),
        P("space"),
        P(),
        P("space"),
        P("space"),
    )
    out_specs = (P("probe", "space", None, None), P("probe", "space", None, None))
    return jax.shard_map(shards, mesh=mesh, in_specs=in_specs, out_specs=out_specs, check_vma=False)
```

```python
import jax
import jax.numpy as jnp
from jax import lax
from jax.experimental import pallas as pl
from jax.experimental.pallas import tpu as pltpu
from jax.sharding import PartitionSpec as P


F32 = jnp.float32
BF16 = jnp.bfloat16
NY, NZ = 32, 256
OWN = 4
EXT = 5 * OWN
LIST = 8
UNROLL = True
VMEM = pl.BlockSpec(memory_space=pltpu.VMEM)
SMEM = pl.BlockSpec(memory_space=pltpu.SMEM)
NT_DIMS = (((1,), (1,)), ((), ()))
NN_DIMS = (((1,), (0,)), ((), ()))


def call(kernel, outs, n_in, scratch=(), smem=(), mib=8):
    shapes = [jax.ShapeDtypeStruct(s, F32) for s in outs]
    return pl.pallas_call(
        kernel,
        out_shape=shapes if len(shapes) > 1 else shapes[0],
        in_specs=[SMEM if i in smem else VMEM for i in range(n_in)],
        out_specs=[VMEM] * len(shapes) if len(shapes) > 1 else VMEM,
        scratch_shapes=list(scratch),
        compiler_params=pltpu.CompilerParams(vmem_limit_bytes=mib << 20),
    )


def core_of():
    return lax.rem(lax.axis_index("space"), 2)


def halves(x):
    hi = x.astype(BF16)
    lo = (x - hi.astype(F32)).astype(BF16)
    return hi, lo


def dot(a, b, dims):
    return lax.dot_general(a, b, dims, preferred_element_type=F32)


def one_hots(cells):
    cell = cells.astype(jnp.int32)
    count = cell.shape[1]
    row = lax.shift_right_logical(cell, 8)
    col = lax.bitwise_and(cell, NZ - 1)
    in_row = lax.broadcasted_iota(jnp.int32, (OWN * NY, count), 0) == row
    in_col = lax.broadcasted_iota(jnp.int32, (NZ, count), 0) == col
    return in_row, in_col.astype(F32).astype(BF16)


def tiles_of(ref, *index):
    return [
        [ref[index + (slice(y, y + 8), slice(z, z + 128))] for z in range(0, NZ, 128)]
        for y in range(0, NY, 8)
    ]


def put_tile(ref, index, j, h, value):
    ref[index + (slice(8 * j, 8 * j + 8), slice(128 * h, 128 * h + 128))] = value


def make_laplace():
    y = lax.broadcasted_iota(jnp.int32, (8, 128), 0)
    z = lax.broadcasted_iota(jnp.int32, (8, 128), 1)
    y_lo, y_hi, z_lo, z_hi = y == 0, y == 7, z == 0, z == 127
    zero = jnp.zeros((8, 128), F32)

    def laplace(below, f, above):
        rows, cols = len(f), len(f[0])

        def shifted(axis, by):
            return [[pltpu.roll(v, by, axis) for v in line] for line in f]

        up, down, left, right = shifted(0, 1), shifted(0, 7), shifted(1, 1), shifted(1, 127)
        out = []
        for j in range(rows):
            line = []
            for h in range(cols):
                total = below[j][h] + above[j][h]
                side = jnp.where(y_lo, up[j - 1][h] if j > 0 else zero, up[j][h])
                total = total + side
                side = jnp.where(y_hi, down[j + 1][h] if j + 1 < rows else zero, down[j][h])
                total = total + side
                side = jnp.where(z_lo, left[j][h - 1] if h > 0 else zero, left[j][h])
                total = total + side
                side = jnp.where(z_hi, right[j][h + 1] if h + 1 < cols else zero, right[j][h])
                total = total + side
                line.append(total - 6.0 * f[j][h])
            out.append(line)
        return out

    return laplace


TILES = [(j, h) for j in range(NY // 8) for h in range(NZ // 128)]


def pack(src, strength, rec, weight, out):
    chip_cell = (lax.axis_index("space") // 2) * (OWN * NY * NZ)
    out[...] = jnp.zeros((LIST, NZ), F32)
    out[0:1, 0:64] = (src[...] - chip_cell).astype(F32)
    out[1:2, 0:64] = strength[...]
    out[2:3, 0:64] = (rec[...] - chip_cell).astype(F32)
    out[3:4, 0:64] = weight[...]


def both_lists(own, got, core):
    first = core == 0
    low = jnp.where(first, own, got)
    high = jnp.where(first, got, own)
    return low[:, 0:128] + pltpu.roll(high[:, 0:128], 64, 1)


def forward(
    p,
    p_got,
    c_own,
    c_got,
    lists,
    lists_got,
    near,
    far,
    near_got,
    far_got,
    near_p,
    far_p,
    wavelet,
    drives,
    wrec,
    courant,
    cells,
    src,
    wave,
    born,
    probe,
    drive,
    table,
):
    core = core_of()
    back = 1 - core
    chip = lax.axis_index("space") // 2
    last = lax.axis_size("space") // 2 - 1
    lo1, lo2 = chip >= 1, chip >= 2
    hi1, hi2 = chip <= last - 1, chip <= last - 2
    first = core == 0

    def factor(ok):
        return jnp.where(ok, 1.0, 0.0).astype(F32)

    keep_near = factor(jnp.where(first, lo1, hi1))
    keep_far = factor(jnp.where(first, lo2, hi2))
    keep_near_got = factor(jnp.where(first, hi1, lo1))
    keep_far_got = factor(jnp.where(first, hi2, lo2))
    one = jnp.float32(1.0)

    def put_list(slot, low, high, side, scale):
        listed = both_lists(low, high, side)
        at = pl.multiple_of(slot * LIST, LIST)
        table[pl.ds(at, LIST), :] = listed
        table[pl.ds(at + 1, 1), :] = scale * listed[1:2]

    put_list(2, lists[...], lists_got[...], core, one)
    put_list(1 + 2 * core, near[384:392, :], near[392:400, :], core, keep_near)
    put_list(3 - 2 * core, near_got[384:392, :], near_got[392:400, :], back, keep_near_got)
    put_list(4 * core, far[192:200, :], far[200:208, :], core, keep_far)
    put_list(4 - 4 * core, far_got[192:200, :], far_got[200:208, :], back, keep_far_got)

    def put_probe(at, ref, row):
        for i in range(2):
            piece = ref[row + 64 * i : row + 64 * (i + 1), :]
            probe[i, pl.ds(at, 2)] = piece.reshape(2, NY, NZ)

    def put_courant(at, ref, row, scale):
        courant[pl.ds(at, 2)] = scale * ref[row : row + 64, :].reshape(2, NY, NZ)

    for i in range(2):
        probe[i, pl.ds(8 + 2 * core, 2)] = p[2 * core + i]
        probe[i, pl.ds(8 + 2 * back, 2)] = p_got[2 * core + i]
    courant[pl.ds(8 + 2 * core, 2)] = c_own[...]
    courant[pl.ds(8 + 2 * back, 2)] = c_got[...]
    base, base_got = 4 + 8 * core, 12 - 8 * core
    put_probe(base + 2 * core, near_p, 0)
    put_probe(base + 2 * back, near_p, 128)
    put_probe(base_got + 2 * back, near_got, 0)
    put_probe(base_got + 2 * core, near_got, 128)
    put_probe(2 + 14 * core, far_p, 0)
    put_probe(16 - 14 * core, far_got, 0)
    put_courant(base + 2 * core, near, 256, keep_near)
    put_courant(base + 2 * back, near, 320, keep_near)
    put_courant(base_got + 2 * back, near_got, 256, keep_near_got)
    put_courant(base_got + 2 * core, near_got, 320, keep_near_got)
    put_courant(2 + 14 * core, far, 128, keep_far)
    put_courant(16 - 14 * core, far_got, 128, keep_far_got)
    zero = jnp.zeros((NY, NZ), F32)
    for e in (0, 1, 18, 19):
        courant[e] = zero
    cells[...] = jnp.zeros((LIST, 128), F32)
    for m in range(5):
        listed = table[LIST * m : LIST * (m + 1), :]
        in_row, in_col = one_hots(listed[0:1])
        hi, lo = halves(jnp.where(in_row, listed[1:2], 0.0))
        field = dot(hi, in_col, NT_DIMS) + dot(lo, in_col, NT_DIMS)
        src[4 * m : 4 * m + 4] = field.reshape(OWN, NY, NZ)
        cells[m : m + 1, :] = listed[2:3]
    pulse_0 = wavelet[0]

    def start(e, _):
        wave[1, e] = pulse_0 * src[e]
        wave[0, e] = zero
        for i in range(2):
            born[0, i, e] = zero
            born[1, i, e] = zero
        return 0

    lax.fori_loop(0, EXT, start, 0)
    laplace = make_laplace()
    listed = table[2 * LIST : 3 * LIST, :]
    in_row, in_col = one_hots(listed[2:3])
    row_mask = jnp.where(in_row, 1.0, 0.0)
    weight = listed[3:4]
    wrec[...] = jnp.zeros((16, 128), F32)
    for t in range(1, 8):
        now, nxt = t % 2, (t + 1) % 2
        pulse = wavelet[t]

        def advance(e, _, now=now, nxt=nxt, pulse=pulse, t=t):
            c = tiles_of(courant, e)
            w = tiles_of(wave, now, e)
            d = laplace(tiles_of(wave, now, e - 1), w, tiles_of(wave, now, e + 1))
            for j, h in TILES:
                d[j][h] = c[j][h] * d[j][h]
                put_tile(drive, (e,), j, h, d[j][h])
            if t < 7:
                w_old, s = tiles_of(wave, nxt, e), tiles_of(src, e)
                for j, h in TILES:
                    w_new = 2.0 * w[j][h] - w_old[j][h] + d[j][h] + pulse * s[j][h]
                    put_tile(wave, (nxt, e), j, h, w_new)
            for i in range(2):
                q = tiles_of(probe, i, e)
                if t > 1:
                    b = tiles_of(born, now, i, e)
                    bent = laplace(
                        tiles_of(born, now, i, e - 1), b, tiles_of(born, now, i, e + 1)
                    )
                    b_old = tiles_of(born, nxt, i, e)
                for j, h in TILES:
                    b_new = q[j][h] * d[j][h]
                    if t > 1:
                        moved = 2.0 * b[j][h] - b_old[j][h] + c[j][h] * bent[j][h]
                        b_new = b_new + moved
                    put_tile(born, (nxt, i, e), j, h, b_new)
            return 0

        lax.fori_loop(1 + t, 19 - t, advance, 0, unroll=UNROLL)
        drives[t - 1] = drive[8:12]
        for i in range(2):
            hi, lo = halves(born[nxt, i, 8:12].reshape(OWN * NY, NZ))
            picked = dot(hi, in_col, NN_DIMS) + dot(lo, in_col, NN_DIMS)
            value = jnp.sum(picked * row_mask, axis=0, keepdims=True)
            at = 2 * (t - 1) + i
            wrec[at : at + 1, :] = value * weight


def adjoint(
    courant, cells, w0, near, far, near_got, far_got, drives, mine, send, inj, adj, bent, hess
):
    first = core_of() == 0
    side = [near[0:16, :], near_got[16:32, :], far[0:16, :], far_got[16:32, :]]
    recs = (
        jnp.where(first, side[2], side[3]),
        jnp.where(first, side[0], side[1]),
        w0[...],
        jnp.where(first, side[1], side[0]),
        jnp.where(first, side[3], side[2]),
    )
    for m, rec in enumerate(recs):
        in_row, in_col = one_hots(cells[m : m + 1, :])
        for k in range(8, 1, -1):
            lo_e, hi_e = 10 - k, 9 + k
            if 4 * m + 3 < lo_e or 4 * m > hi_e:
                continue
            for i in range(2):
                at = 2 * (k - 2) + i
                hi, lo = halves(rec[at : at + 1, :])
                a = jnp.where(in_row, hi.astype(F32), 0.0).astype(BF16)
                b = jnp.where(in_row, lo.astype(F32), 0.0).astype(BF16)
                field = dot(a, in_col, NT_DIMS) + dot(b, in_col, NT_DIMS)
                inj[k - 2, i, 4 * m : 4 * m + 4] = field.reshape(OWN, NY, NZ)
    laplace = make_laplace()

    def begin(e, _):
        for i in range(2):
            a = inj[6, i, e]
            adj[0, i, e] = a
            bent[0, i, e] = courant[e] * a
        return 0

    lax.fori_loop(2, 18, begin, 0)
    for i in range(2):
        for e in range(OWN):
            hess[i, e] = drives[6, e] * adj[0, i, 8 + e]
    for k in range(7, 1, -1):
        now, nxt = k % 2, (k + 1) % 2

        def advance(e, _, k=k, now=now, nxt=nxt):
            c = tiles_of(courant, e)
            for i in range(2):
                a_new = laplace(
                    tiles_of(bent, nxt, i, e - 1),
                    tiles_of(bent, nxt, i, e),
                    tiles_of(bent, nxt, i, e + 1),
                )
                a, a_old = tiles_of(adj, nxt, i, e), tiles_of(adj, now, i, e)
                pushed = tiles_of(inj, k - 2, i, e)
                for j, h in TILES:
                    value = a_new[j][h] + (2.0 * a[j][h] + pushed[j][h])
                    if k < 7:
                        value = value - a_old[j][h]
                    put_tile(adj, (now, i, e), j, h, value)
                    if k > 2:
                        put_tile(bent, (now, i, e), j, h, c[j][h] * value)
            return 0

        lax.fori_loop(10 - k, 10 + k, advance, 0, unroll=UNROLL)
        for i in range(2):
            for e in range(OWN):
                hess[i, e] = hess[i, e] + drives[k - 2, e] * adj[now, i, 8 + e]
    core = core_of()
    for i in range(2):
        for e in range(2):
            mine[i, e] = hess[i, 2 * core + e]
            send[i, e] = hess[i, 2 * (1 - core) + e]


def finish(p, prior, mine, got, out, low, high):
    core = core_of()
    for i in range(2):
        out[2 * core + i] = prior[...] * p[2 * core + i] + mine[i]
        out[2 * (1 - core) + i] = prior[...] * p[2 * (1 - core) + i] + got[i]
    low[...] = out[0:2]
    high[...] = out[2:4]


def gram_part(*refs):
    *rows, out, sums = refs
    group = lax.axis_index("probe")
    start = [lax.rem(group + 4 - b, 4) * 4 for b in range(4)]
    for a in range(4):
        for b in range(a, 4):
            pairs = [(i, j) for i in range(4) for j in range(4) if a != b or i <= j]
            acc = [None] * len(pairs)
            for plane in range(2):
                for y in range(0, NY, 8):
                    left = [rows[2 * a + i // 2][i % 2, plane, y : y + 8, :] for i in range(4)]
                    right = [rows[2 * b + j // 2][j % 2, plane, y : y + 8, :] for j in range(4)]
                    for n, (i, j) in enumerate(pairs):
                        prod = left[i] * right[j]
                        prod = prod[:, :128] + prod[:, 128:]
                        acc[n] = prod if acc[n] is None else acc[n] + prod
            for n, (i, j) in enumerate(pairs):
                total = jnp.sum(acc[n], axis=0, keepdims=True)
                row, col = start[a] + i, start[b] + j
                sums[pl.ds(row * 16 + col, 1), :] = total
                sums[pl.ds(col * 16 + row, 1), :] = total
    flat = lax.dot_general(
        jnp.ones((8, 128), F32),
        sums[...],
        NT_DIMS,
        precision=lax.Precision.HIGHEST,
        preferred_element_type=F32,
    )
    pair = jnp.concatenate([flat[0:1, :128], flat[0:1, 128:]], axis=0)
    out[...] = jnp.broadcast_to(pair[None], out.shape)


def whiten(scale, parts, *refs):
    *rows, out, work = refs
    exact = dict(precision=lax.Precision.HIGHEST, preferred_element_type=F32)
    group = lax.axis_index("probe")
    total = jnp.sum(parts[...], axis=0) * scale
    row = lax.broadcasted_iota(jnp.int32, (16, 128), 0)
    lane = lax.broadcasted_iota(jnp.int32, (16, 128), 1)
    spread = jnp.where(
        row < 8,
        jnp.broadcast_to(total[0:1], (16, 128)),
        jnp.broadcast_to(total[1:2], (16, 128)),
    )
    spread = jnp.where(lax.shift_right_logical(lane, 4) == lax.bitwise_and(row, 7), spread, 0.0)
    from_lane = lax.broadcasted_iota(jnp.int32, (128, 128), 0)
    to_lane = lax.broadcasted_iota(jnp.int32, (128, 128), 1)
    select = jnp.where(lax.bitwise_and(from_lane, 15) == to_lane, 1.0, 0.0)
    x = lax.dot_general(spread, select, NN_DIMS, **exact)
    x = x + jnp.where(lane == row + 16, 1.0, 0.0)
    for k in range(16):
        column = jnp.broadcast_to(x[:, k : k + 1], (16, 128))
        pivot = jnp.broadcast_to(column[k : k + 1], (16, 128))
        ratio = jnp.broadcast_to(x[k : k + 1], (16, 128)) / pivot
        x = jnp.where(row > k, x - column * ratio, x)
        x = jnp.where(row == k, x * lax.rsqrt(pivot), x)
    work[...] = x
    picked = work[pl.ds(pl.multiple_of(group * 4, 4), 4), :]
    picked = jnp.concatenate([picked, picked], axis=0)
    block = lax.bitwise_and(group + 4 - lax.shift_right_logical(to_lane, 2), 3)
    source = 16 + block * 4 + lax.bitwise_and(to_lane, 3)
    order = jnp.where(jnp.logical_and(from_lane == source, to_lane < 16), 1.0, 0.0)
    coef = lax.dot_general(picked, order, NN_DIMS, **exact)
    for r in range(4):
        c = [jnp.broadcast_to(coef[r : r + 1, s : s + 1], (8, NZ)) for s in range(16)]
        for plane in range(2):
            for y in range(0, NY, 8):
                acc = None
                for s in range(16):
                    term = c[s] * rows[s // 2][s % 2, plane, y : y + 8, :]
                    acc = term if acc is None else acc + term
                out[r, plane, y : y + 8, :] = acc


def shards(
    courant_field,
    probe_fields,
    prior_weight,
    source_cells,
    source_strength,
    wavelet,
    receiver_cells,
    receiver_weight,
):
    count = lax.axis_size("space")

    def swap(x):
        return lax.ppermute(x, "space", [(i, i ^ 1) for i in range(count)])

    def inward(x, by):
        pairs = [(i, (i + (by if i % 2 == 0 else -by)) % count) for i in range(count)]
        return lax.ppermute(x, "space", pairs)

    p = probe_fields
    core = core_of()
    p_got, c_got = swap(p), swap(courant_field)
    lists = call(pack, [(LIST, NZ)], 4)(
        *[
            v.reshape(1, -1)
            for v in (source_cells, source_strength, receiver_cells, receiver_weight)
        ]
    )
    lists_got = swap(lists)

    def pair_of(x, side):
        return lax.dynamic_slice_in_dim(x, 2 * side, 2, 0).reshape(128, NZ)

    c_rows, c_got_rows = courant_field.reshape(64, NZ), c_got.reshape(64, NZ)
    rest = jnp.concatenate([pair_of(p, core), pair_of(p_got, core)], axis=0)
    near = inward(
        jnp.concatenate(
            [pair_of(p, 1 - core), pair_of(p_got, 1 - core), c_rows, c_got_rows, lists, lists_got],
            axis=0,
        ),
        2,
    )
    far = inward(
        jnp.concatenate(
            [pair_of(p_got, 1 - core), c_got_rows, lists, lists_got], axis=0
        ),
        4,
    )
    near_p = inward(rest, 2)
    far_p = inward(pair_of(p_got, core), 4)
    near_got = swap(near)
    far_got = swap(far)
    plane = (NY, NZ)
    drives, wrec, courant, cells = call(
        forward,
        [(7, OWN) + plane, (16, 128), (EXT,) + plane, (LIST, 128)],
        13,
        scratch=[
            pltpu.VMEM((EXT,) + plane, F32),
            pltpu.VMEM((2, EXT) + plane, F32),
            pltpu.VMEM((2, 2, EXT) + plane, F32),
            pltpu.VMEM((2, EXT) + plane, F32),
            pltpu.VMEM((EXT,) + plane, F32),
            pltpu.VMEM((5 * LIST, 128), F32),
        ],
        smem=(12,),
        mib=16,
    )(
        p,
        p_got,
        courant_field,
        c_got,
        lists,
        lists_got,
        near,
        far,
        near_got,
        far_got,
        near_p,
        far_p,
        wavelet,
    )
    all_rec = jnp.concatenate([wrec, swap(wrec)], axis=0)
    rec_near, rec_far = inward(all_rec, 2), inward(all_rec, 4)
    rec_near_got, rec_far_got = swap(rec_near), swap(rec_far)
    half = (2, 2) + plane
    mine, send = call(
        adjoint,
        [half, half],
        8,
        scratch=[
            pltpu.VMEM((7, 2, EXT) + plane, F32),
            pltpu.VMEM((2, 2, EXT) + plane, F32),
            pltpu.VMEM((2, 2, EXT) + plane, F32),
            pltpu.VMEM((2, OWN) + plane, F32),
        ],
        mib=24,
    )(courant, cells, wrec, rec_near, rec_far, rec_near_got, rec_far_got, drives)
    hessian, low, high = call(finish, [(4, 2) + plane, half, half], 4)(
        probe_fields, prior_weight, mine, swap(send)
    )
    groups = lax.axis_size("probe")

    def turn(x, by):
        return lax.ppermute(x, "probe", [(i, (i + by) % groups) for i in range(groups)])

    low_1, high_3 = turn(low, 1), turn(high, -1)
    high_1, low_3 = turn(high, 1), turn(low, -1)
    low_2, high_2 = turn(low_1, 1), turn(high_3, -1)
    rows = [low, high, low_1, high_1, low_2, high_2, low_3, high_3]
    part = call(gram_part, [(count, 2, 128)], 8, scratch=[pltpu.VMEM((256, 128), F32)])(*rows)
    parts = lax.all_to_all(part, "space", 0, 0, tiled=True)
    scale = 1.0 / (count * hessian[0].size)

    def whiten_scaled(*refs):
        whiten(scale, *refs)

    basis = call(
        whiten_scaled, [(4, 2) + plane], 9, scratch=[pltpu.VMEM((16, 128), F32)]
    )(parts, *rows)
    return (hessian, basis)


def solution(mesh):
    in_specs = (
        P("space", None, None),
        P("probe", "space", None, None),
        P("space", None, None),
        P("space"),
        P("space"),
        P(),
        P("space"),
        P("space"),
    )
    out_specs = (P("probe", "space", None, None), P("probe", "space", None, None))
    return jax.shard_map(shards, mesh=mesh, in_specs=in_specs, out_specs=out_specs, check_vma=False)
```

```python
import jax
import jax.numpy as jnp
from jax import lax
from jax.experimental import pallas as pl
from jax.experimental.pallas import tpu as pltpu
from jax.sharding import PartitionSpec as P


F32 = jnp.float32
BF16 = jnp.bfloat16
NY, NZ = 32, 256
OWN = 4
EXT = 5 * OWN
LIST = 8
UNROLL = True
VMEM = pl.BlockSpec(memory_space=pltpu.VMEM)
SMEM = pl.BlockSpec(memory_space=pltpu.SMEM)
NT_DIMS = (((1,), (1,)), ((), ()))
NN_DIMS = (((1,), (0,)), ((), ()))


def call(kernel, outs, n_in, scratch=(), smem=(), mib=8):
    shapes = [jax.ShapeDtypeStruct(s, F32) for s in outs]
    return pl.pallas_call(
        kernel,
        out_shape=shapes if len(shapes) > 1 else shapes[0],
        in_specs=[SMEM if i in smem else VMEM for i in range(n_in)],
        out_specs=[VMEM] * len(shapes) if len(shapes) > 1 else VMEM,
        scratch_shapes=list(scratch),
        compiler_params=pltpu.CompilerParams(vmem_limit_bytes=mib << 20),
    )


def core_of():
    return lax.rem(lax.axis_index("space"), 2)


def halves(x):
    hi = x.astype(BF16)
    lo = (x - hi.astype(F32)).astype(BF16)
    return hi, lo


def dot(a, b, dims):
    return lax.dot_general(a, b, dims, preferred_element_type=F32)


def one_hots(cells):
    cell = cells.astype(jnp.int32)
    count = cell.shape[1]
    row = lax.shift_right_logical(cell, 8)
    col = lax.bitwise_and(cell, NZ - 1)
    in_row = lax.broadcasted_iota(jnp.int32, (OWN * NY, count), 0) == row
    in_col = lax.broadcasted_iota(jnp.int32, (NZ, count), 0) == col
    return in_row, in_col.astype(F32).astype(BF16)


def tiles_of(ref, *index):
    return [
        [ref[index + (slice(y, y + 8), slice(z, z + 128))] for z in range(0, NZ, 128)]
        for y in range(0, NY, 8)
    ]


def put_tile(ref, index, j, h, value):
    ref[index + (slice(8 * j, 8 * j + 8), slice(128 * h, 128 * h + 128))] = value


def make_laplace():
    y = lax.broadcasted_iota(jnp.int32, (8, 128), 0)
    z = lax.broadcasted_iota(jnp.int32, (8, 128), 1)
    y_lo, y_hi, z_lo, z_hi = y == 0, y == 7, z == 0, z == 127
    zero = jnp.zeros((8, 128), F32)

    def laplace(below, f, above):
        rows, cols = len(f), len(f[0])

        def shifted(axis, by):
            return [[pltpu.roll(v, by, axis) for v in line] for line in f]

        up, down, left, right = shifted(0, 1), shifted(0, 7), shifted(1, 1), shifted(1, 127)
        out = []
        for j in range(rows):
            line = []
            for h in range(cols):
                total = below[j][h] + above[j][h]
                side = jnp.where(y_lo, up[j - 1][h] if j > 0 else zero, up[j][h])
                total = total + side
                side = jnp.where(y_hi, down[j + 1][h] if j + 1 < rows else zero, down[j][h])
                total = total + side
                side = jnp.where(z_lo, left[j][h - 1] if h > 0 else zero, left[j][h])
                total = total + side
                side = jnp.where(z_hi, right[j][h + 1] if h + 1 < cols else zero, right[j][h])
                total = total + side
                line.append(total - 6.0 * f[j][h])
            out.append(line)
        return out

    return laplace


TILES = [(j, h) for j in range(NY // 8) for h in range(NZ // 128)]


def pack(src, strength, rec, weight, out):
    chip_cell = (lax.axis_index("space") // 2) * (OWN * NY * NZ)
    out[...] = jnp.zeros((LIST, NZ), F32)
    out[0:1, 0:64] = (src[...] - chip_cell).astype(F32)
    out[1:2, 0:64] = strength[...]
    out[2:3, 0:64] = (rec[...] - chip_cell).astype(F32)
    out[3:4, 0:64] = weight[...]


def both_lists(own, got, core):
    first = core == 0
    low = jnp.where(first, own, got)
    high = jnp.where(first, got, own)
    return low[:, 0:128] + pltpu.roll(high[:, 0:128], 64, 1)


def forward(
    p,
    p_got,
    c_own,
    c_got,
    lists,
    lists_got,
    near,
    far,
    near_got,
    far_got,
    near_p,
    far_p,
    wavelet,
    drives,
    wrec,
    courant,
    cells,
    src,
    wave,
    born,
    probe,
    drive,
    table,
):
    core = core_of()
    back = 1 - core
    chip = lax.axis_index("space") // 2
    last = lax.axis_size("space") // 2 - 1
    lo1, lo2 = chip >= 1, chip >= 2
    hi1, hi2 = chip <= last - 1, chip <= last - 2
    first = core == 0

    def factor(ok):
        return jnp.where(ok, 1.0, 0.0).astype(F32)

    keep_near = factor(jnp.where(first, lo1, hi1))
    keep_far = factor(jnp.where(first, lo2, hi2))
    keep_near_got = factor(jnp.where(first, hi1, lo1))
    keep_far_got = factor(jnp.where(first, hi2, lo2))
    one = jnp.float32(1.0)

    def put_list(slot, low, high, side, scale):
        listed = both_lists(low, high, side)
        at = pl.multiple_of(slot * LIST, LIST)
        table[pl.ds(at, LIST), :] = listed
        table[pl.ds(at + 1, 1), :] = scale * listed[1:2]

    put_list(2, lists[...], lists_got[...], core, one)
    put_list(1 + 2 * core, near[384:392, :], near[392:400, :], core, keep_near)
    put_list(3 - 2 * core, near_got[384:392, :], near_got[392:400, :], back, keep_near_got)
    put_list(4 * core, far[192:200, :], far[200:208, :], core, keep_far)
    put_list(4 - 4 * core, far_got[192:200, :], far_got[200:208, :], back, keep_far_got)

    def put_probe(at, ref, row):
        for i in range(2):
            piece = ref[row + 64 * i : row + 64 * (i + 1), :]
            probe[i, pl.ds(at, 2)] = piece.reshape(2, NY, NZ)

    def put_courant(at, ref, row, scale):
        courant[pl.ds(at, 2)] = scale * ref[row : row + 64, :].reshape(2, NY, NZ)

    for i in range(2):
        probe[i, pl.ds(8 + 2 * core, 2)] = p[2 * core + i]
        probe[i, pl.ds(8 + 2 * back, 2)] = p_got[2 * core + i]
    courant[pl.ds(8 + 2 * core, 2)] = c_own[...]
    courant[pl.ds(8 + 2 * back, 2)] = c_got[...]
    base, base_got = 4 + 8 * core, 12 - 8 * core
    put_probe(base + 2 * core, near_p, 0)
    put_probe(base + 2 * back, near_p, 128)
    put_probe(base_got + 2 * back, near_got, 0)
    put_probe(base_got + 2 * core, near_got, 128)
    put_probe(2 + 14 * core, far_p, 0)
    put_probe(16 - 14 * core, far_got, 0)
    put_courant(base + 2 * core, near, 256, keep_near)
    put_courant(base + 2 * back, near, 320, keep_near)
    put_courant(base_got + 2 * back, near_got, 256, keep_near_got)
    put_courant(base_got + 2 * core, near_got, 320, keep_near_got)
    put_courant(2 + 14 * core, far, 128, keep_far)
    put_courant(16 - 14 * core, far_got, 128, keep_far_got)
    zero = jnp.zeros((NY, NZ), F32)
    for e in (0, 1, 18, 19):
        courant[e] = zero
    cells[...] = jnp.zeros((LIST, 128), F32)
    for m in range(5):
        listed = table[LIST * m : LIST * (m + 1), :]
        in_row, in_col = one_hots(listed[0:1])
        hi, lo = halves(jnp.where(in_row, listed[1:2], 0.0))
        field = dot(hi, in_col, NT_DIMS) + dot(lo, in_col, NT_DIMS)
        src[4 * m : 4 * m + 4] = field.reshape(OWN, NY, NZ)
        cells[m : m + 1, :] = listed[2:3]
    pulse_0 = wavelet[0]

    def start(e, _):
        wave[1, e] = pulse_0 * src[e]
        wave[0, e] = zero
        for i in range(2):
            born[0, i, e] = zero
            born[1, i, e] = zero
        return 0

    lax.fori_loop(0, EXT, start, 0)
    laplace = make_laplace()
    listed = table[2 * LIST : 3 * LIST, :]
    in_row, in_col = one_hots(listed[2:3])
    row_mask = jnp.where(in_row, 1.0, 0.0)
    weight = listed[3:4]
    wrec[...] = jnp.zeros((16, 128), F32)
    for t in range(1, 8):
        now, nxt = t % 2, (t + 1) % 2
        pulse = wavelet[t]

        def advance(e, _, now=now, nxt=nxt, pulse=pulse, t=t):
            c = tiles_of(courant, e)
            w = tiles_of(wave, now, e)
            d = laplace(tiles_of(wave, now, e - 1), w, tiles_of(wave, now, e + 1))
            for j, h in TILES:
                d[j][h] = c[j][h] * d[j][h]
                put_tile(drive, (e,), j, h, d[j][h])
            if t < 7:
                w_old, s = tiles_of(wave, nxt, e), tiles_of(src, e)
                for j, h in TILES:
                    w_new = 2.0 * w[j][h] - w_old[j][h] + d[j][h] + pulse * s[j][h]
                    put_tile(wave, (nxt, e), j, h, w_new)
            for i in range(2):
                q = tiles_of(probe, i, e)
                if t > 1:
                    b = tiles_of(born, now, i, e)
                    bent = laplace(
                        tiles_of(born, now, i, e - 1), b, tiles_of(born, now, i, e + 1)
                    )
                    b_old = tiles_of(born, nxt, i, e)
                for j, h in TILES:
                    b_new = q[j][h] * d[j][h]
                    if t > 1:
                        moved = 2.0 * b[j][h] - b_old[j][h] + c[j][h] * bent[j][h]
                        b_new = b_new + moved
                    put_tile(born, (nxt, i, e), j, h, b_new)
            return 0

        lax.fori_loop(1 + t, 19 - t, advance, 0, unroll=UNROLL)
        drives[t - 1] = drive[8:12]
        for i in range(2):
            hi, lo = halves(born[nxt, i, 8:12].reshape(OWN * NY, NZ))
            picked = dot(hi, in_col, NN_DIMS) + dot(lo, in_col, NN_DIMS)
            value = jnp.sum(picked * row_mask, axis=0, keepdims=True)
            at = 2 * (t - 1) + i
            wrec[at : at + 1, :] = value * weight


def adjoint(
    courant, cells, w0, near, far, near_got, far_got, drives, mine, send, inj, adj, bent, hess
):
    first = core_of() == 0
    side = [near[0:16, :], near_got[16:32, :], far[0:16, :], far_got[16:32, :]]
    recs = (
        jnp.where(first, side[2], side[3]),
        jnp.where(first, side[0], side[1]),
        w0[...],
        jnp.where(first, side[1], side[0]),
        jnp.where(first, side[3], side[2]),
    )
    for m, rec in enumerate(recs):
        in_row, in_col = one_hots(cells[m : m + 1, :])
        for k in range(8, 1, -1):
            lo_e, hi_e = 10 - k, 9 + k
            if 4 * m + 3 < lo_e or 4 * m > hi_e:
                continue
            for i in range(2):
                at = 2 * (k - 2) + i
                hi, lo = halves(rec[at : at + 1, :])
                a = jnp.where(in_row, hi.astype(F32), 0.0).astype(BF16)
                b = jnp.where(in_row, lo.astype(F32), 0.0).astype(BF16)
                field = dot(a, in_col, NT_DIMS) + dot(b, in_col, NT_DIMS)
                inj[k - 2, i, 4 * m : 4 * m + 4] = field.reshape(OWN, NY, NZ)
    laplace = make_laplace()

    def begin(e, _):
        for i in range(2):
            a = inj[6, i, e]
            adj[0, i, e] = a
            bent[0, i, e] = courant[e] * a
        return 0

    lax.fori_loop(2, 18, begin, 0)
    for i in range(2):
        for e in range(OWN):
            hess[i, e] = drives[6, e] * adj[0, i, 8 + e]
    for k in range(7, 1, -1):
        now, nxt = k % 2, (k + 1) % 2

        def advance(e, _, k=k, now=now, nxt=nxt):
            c = tiles_of(courant, e)
            for i in range(2):
                a_new = laplace(
                    tiles_of(bent, nxt, i, e - 1),
                    tiles_of(bent, nxt, i, e),
                    tiles_of(bent, nxt, i, e + 1),
                )
                a, a_old = tiles_of(adj, nxt, i, e), tiles_of(adj, now, i, e)
                pushed = tiles_of(inj, k - 2, i, e)
                for j, h in TILES:
                    value = a_new[j][h] + (2.0 * a[j][h] + pushed[j][h])
                    if k < 7:
                        value = value - a_old[j][h]
                    put_tile(adj, (now, i, e), j, h, value)
                    if k > 2:
                        put_tile(bent, (now, i, e), j, h, c[j][h] * value)
            return 0

        lax.fori_loop(10 - k, 10 + k, advance, 0, unroll=UNROLL)
        for i in range(2):
            for e in range(OWN):
                hess[i, e] = hess[i, e] + drives[k - 2, e] * adj[now, i, 8 + e]
    core = core_of()
    for i in range(2):
        for e in range(2):
            mine[i, e] = hess[i, 2 * core + e]
            send[i, e] = hess[i, 2 * (1 - core) + e]


def finish(p, prior, mine, got, out, low, high):
    core = core_of()
    for i in range(2):
        out[2 * core + i] = prior[...] * p[2 * core + i] + mine[i]
        out[2 * (1 - core) + i] = prior[...] * p[2 * (1 - core) + i] + got[i]
    low[...] = out[0:2]
    high[...] = out[2:4]


def gram_part(*refs):
    *rows, out, sums = refs
    group = lax.axis_index("probe")
    start = [lax.rem(group + 4 - b, 4) * 4 for b in range(4)]
    for a in range(4):
        for b in range(a, 4):
            pairs = [(i, j) for i in range(4) for j in range(4) if a != b or i <= j]
            acc = [None] * len(pairs)
            for plane in range(2):
                for y in range(0, NY, 8):
                    left = [rows[2 * a + i // 2][i % 2, plane, y : y + 8, :] for i in range(4)]
                    right = [rows[2 * b + j // 2][j % 2, plane, y : y + 8, :] for j in range(4)]
                    for n, (i, j) in enumerate(pairs):
                        prod = left[i] * right[j]
                        prod = prod[:, :128] + prod[:, 128:]
                        acc[n] = prod if acc[n] is None else acc[n] + prod
            for n, (i, j) in enumerate(pairs):
                total = jnp.sum(acc[n], axis=0, keepdims=True)
                row, col = start[a] + i, start[b] + j
                sums[pl.ds(row * 16 + col, 1), :] = total
                sums[pl.ds(col * 16 + row, 1), :] = total
    flat = lax.dot_general(
        jnp.ones((8, 128), F32),
        sums[...],
        NT_DIMS,
        precision=lax.Precision.HIGHEST,
        preferred_element_type=F32,
    )
    pair = jnp.concatenate([flat[0:1, :128], flat[0:1, 128:]], axis=0)
    out[...] = jnp.broadcast_to(pair[None], out.shape)


def whiten(scale, parts, *refs):
    *rows, out, work = refs
    exact = dict(precision=lax.Precision.HIGHEST, preferred_element_type=F32)
    group = lax.axis_index("probe")
    total = jnp.sum(parts[...], axis=0) * scale
    row = lax.broadcasted_iota(jnp.int32, (16, 128), 0)
    lane = lax.broadcasted_iota(jnp.int32, (16, 128), 1)
    spread = jnp.where(
        row < 8,
        jnp.broadcast_to(total[0:1], (16, 128)),
        jnp.broadcast_to(total[1:2], (16, 128)),
    )
    spread = jnp.where(lax.shift_right_logical(lane, 4) == lax.bitwise_and(row, 7), spread, 0.0)
    from_lane = lax.broadcasted_iota(jnp.int32, (128, 128), 0)
    to_lane = lax.broadcasted_iota(jnp.int32, (128, 128), 1)
    select = jnp.where(lax.bitwise_and(from_lane, 15) == to_lane, 1.0, 0.0)
    x = lax.dot_general(spread, select, NN_DIMS, **exact)
    x = x + jnp.where(lane == row + 16, 1.0, 0.0)
    columns = [jnp.broadcast_to(x[:, k : k + 1], (16, 128)) for k in range(16)]

    def spread_row(v, k):
        return jnp.broadcast_to(v[k : k + 1], (16, 128))

    for k in range(16):
        pivot = spread_row(columns[k], k)
        ratio = jnp.where(row > k, columns[k] / pivot, 0.0)
        for j in range(k + 1, 16):
            columns[j] = columns[j] - ratio * spread_row(columns[k], j)
        x = x - ratio * spread_row(x, k)
        x = jnp.where(row == k, x * lax.rsqrt(pivot), x)
    work[...] = x
    picked = work[pl.ds(pl.multiple_of(group * 4, 4), 4), :]
    picked = jnp.concatenate([picked, picked], axis=0)
    block = lax.bitwise_and(group + 4 - lax.shift_right_logical(to_lane, 2), 3)
    source = 16 + block * 4 + lax.bitwise_and(to_lane, 3)
    order = jnp.where(jnp.logical_and(from_lane == source, to_lane < 16), 1.0, 0.0)
    coef = lax.dot_general(picked, order, NN_DIMS, **exact)
    for r in range(4):
        c = [jnp.broadcast_to(coef[r : r + 1, s : s + 1], (8, NZ)) for s in range(16)]
        for plane in range(2):
            for y in range(0, NY, 8):
                acc = None
                for s in range(16):
                    term = c[s] * rows[s // 2][s % 2, plane, y : y + 8, :]
                    acc = term if acc is None else acc + term
                out[r, plane, y : y + 8, :] = acc


def shards(
    courant_field,
    probe_fields,
    prior_weight,
    source_cells,
    source_strength,
    wavelet,
    receiver_cells,
    receiver_weight,
):
    count = lax.axis_size("space")

    def swap(x):
        return lax.ppermute(x, "space", [(i, i ^ 1) for i in range(count)])

    def inward(x, by):
        pairs = [(i, (i + (by if i % 2 == 0 else -by)) % count) for i in range(count)]
        return lax.ppermute(x, "space", pairs)

    p = probe_fields
    core = core_of()
    p_got, c_got = swap(p), swap(courant_field)
    lists = call(pack, [(LIST, NZ)], 4)(
        *[
            v.reshape(1, -1)
            for v in (source_cells, source_strength, receiver_cells, receiver_weight)
        ]
    )
    lists_got = swap(lists)

    def pair_of(x, side):
        return lax.dynamic_slice_in_dim(x, 2 * side, 2, 0).reshape(128, NZ)

    c_rows, c_got_rows = courant_field.reshape(64, NZ), c_got.reshape(64, NZ)
    rest = jnp.concatenate([pair_of(p, core), pair_of(p_got, core)], axis=0)
    near = inward(
        jnp.concatenate(
            [pair_of(p, 1 - core), pair_of(p_got, 1 - core), c_rows, c_got_rows, lists, lists_got],
            axis=0,
        ),
        2,
    )
    far = inward(
        jnp.concatenate(
            [pair_of(p_got, 1 - core), c_got_rows, lists, lists_got], axis=0
        ),
        4,
    )
    near_p = inward(rest, 2)
    far_p = inward(pair_of(p_got, core), 4)
    near_got = swap(near)
    far_got = swap(far)
    plane = (NY, NZ)
    drives, wrec, courant, cells = call(
        forward,
        [(7, OWN) + plane, (16, 128), (EXT,) + plane, (LIST, 128)],
        13,
        scratch=[
            pltpu.VMEM((EXT,) + plane, F32),
            pltpu.VMEM((2, EXT) + plane, F32),
            pltpu.VMEM((2, 2, EXT) + plane, F32),
            pltpu.VMEM((2, EXT) + plane, F32),
            pltpu.VMEM((EXT,) + plane, F32),
            pltpu.VMEM((5 * LIST, 128), F32),
        ],
        smem=(12,),
        mib=16,
    )(
        p,
        p_got,
        courant_field,
        c_got,
        lists,
        lists_got,
        near,
        far,
        near_got,
        far_got,
        near_p,
        far_p,
        wavelet,
    )
    all_rec = jnp.concatenate([wrec, swap(wrec)], axis=0)
    rec_near = inward(all_rec, 2)
    rec_far = inward(all_rec, 4)
    rec_near_got = swap(rec_near)
    rec_far_got = swap(rec_far)
    half = (2, 2) + plane
    mine, send = call(
        adjoint,
        [half, half],
        8,
        scratch=[
            pltpu.VMEM((7, 2, EXT) + plane, F32),
            pltpu.VMEM((2, 2, EXT) + plane, F32),
            pltpu.VMEM((2, 2, EXT) + plane, F32),
            pltpu.VMEM((2, OWN) + plane, F32),
        ],
        mib=24,
    )(courant, cells, wrec, rec_near, rec_far, rec_near_got, rec_far_got, drives)
    hessian, low, high = call(finish, [(4, 2) + plane, half, half], 4)(
        probe_fields, prior_weight, mine, swap(send)
    )
    groups = lax.axis_size("probe")

    def turn(x, by):
        return lax.ppermute(x, "probe", [(i, (i + by) % groups) for i in range(groups)])

    low_1, high_3 = turn(low, 1), turn(high, -1)
    high_1, low_3 = turn(high, 1), turn(low, -1)
    low_2, high_2 = turn(low_1, 1), turn(high_3, -1)
    rows = [low, high, low_1, high_1, low_2, high_2, low_3, high_3]
    part = call(gram_part, [(count, 2, 128)], 8, scratch=[pltpu.VMEM((256, 128), F32)])(*rows)
    parts = lax.all_to_all(part, "space", 0, 0, tiled=True)
    scale = 1.0 / (count * hessian[0].size)

    def whiten_scaled(*refs):
        whiten(scale, *refs)

    basis = call(
        whiten_scaled, [(4, 2) + plane], 9, scratch=[pltpu.VMEM((16, 128), F32)]
    )(parts, *rows)
    return (hessian, basis)


def solution(mesh):
    in_specs = (
        P("space", None, None),
        P("probe", "space", None, None),
        P("space", None, None),
        P("space"),
        P("space"),
        P(),
        P("space"),
        P("space"),
    )
    out_specs = (P("probe", "space", None, None), P("probe", "space", None, None))
    return jax.shard_map(shards, mesh=mesh, in_specs=in_specs, out_specs=out_specs, check_vma=False)
```
